256 devices in a mesh: own: 32 (over x_lo, z, core), blk: 8 (over x_hi, y).
Axes of the slice: x: 4 (x_hi: 2, x_lo: 2; x = x_hi * 2 + x_lo), y: 4, z: 8, core: 2. Of those that a mesh axis runs over, the one named last changes fastest.
Arguments:
- amplitudes: bfloat16 [32, 3072, 3072], P('own', 'blk'), may hold values from -6 to 6
- amp_mask: int32 [32, 24, 24], P('own', 'blk'), may hold values 0 or 1
- bare_ints: bfloat16 [32, 3072, 3072], P('own', 'blk'), may hold values from -6 to 6
- int_tiles: bfloat16 [8, 32, 10, 128, 128], P('blk', 'own'), may hold values from -0.125 to 0.125
- tile_ids: int32 [8, 32, 10], P('blk', 'own'), may hold values from -1 to 71, as said below
- eps_virt: float32 [3072], replicated, may hold values from 0.5 to 3
- eps_pair: float32 [32], P('own'), may hold values from -2 to -0.5
Outputs:
- new_amps: bfloat16 [32, 3072, 3072], P('own', 'blk')
The draws below stay inside these ranges and needn't reach their ends.
Inputs may be any that keep to these rules, and one draw needn't show every extreme that they name: `tile_ids`: each entry is -1 or id = a * 24 + c for a live tile at row a of the block's 3 tile rows and column c; each position appears at most once in a block; each block of index g has exactly 64 live tiles, among them always the last position; no device holds more than 10, and in every block one device holds exactly 10.
All inputs are finite; a program needn't handle non-finite values. No bound on the sum of `amp_mask` on one device may be relied on, other than what follows from the above.
Results may differ from the reference program's by a relative error of at most 0.001.
Values may be sent and summed in bfloat16 or wider, within the bound.
A program may use at most 128 MiB of HBM per device.

```python
import jax
import jax.numpy as jnp
from jax import lax

TILE = 128
NT = 24
OWN_CAP = 10
NV = 3072
LIVE = 64
NPAIR = 32
N_OWN = 32
N_BLK = 8


def draw_tile_ids(key, part):
    row_tiles = NT // N_BLK
    positions_all = row_tiles * NT
    others = (N_OWN - 1) * OWN_CAP

    def one_block(block_key):
        key_pos, key_heavy, key_slots, key_mix = jax.random.split(block_key, 4)
        rest_pos = jax.random.permutation(key_pos, positions_all - 1)[:LIVE - 1].astype(jnp.int32)
        last_pos = jnp.full((1,), positions_all - 1, jnp.int32)
        picked = jax.random.permutation(key_mix, jnp.concatenate([last_pos, rest_pos], axis=0)).astype(jnp.int32)
        heavy = jax.random.randint(key_heavy, (), 0, N_OWN).astype(jnp.int32)
        chosen = jax.random.permutation(key_slots, others)[:LIVE - OWN_CAP]
        rest = jnp.full((others,), -1, jnp.int32).at[chosen].set(picked[OWN_CAP:])
        rows = jnp.concatenate([picked[:OWN_CAP][None, :], rest.reshape(N_OWN - 1, OWN_CAP)], axis=0)
        order = (jnp.arange(N_OWN, dtype=jnp.int32) - heavy) % N_OWN
        return rows[order]
    return jax.vmap(one_block)(jax.random.split(key, N_BLK))


def set_ends(values, stream_key, least, largest):
    longest = values.shape.index(max(values.shape))
    spots = []
    for shift in (0, 1):
        where = [jax.random.randint(jax.random.fold_in(stream_key, axis), (), 0, length) for axis, length in enumerate(values.shape)]
        where[longest] = (where[longest] + shift) % values.shape[longest]
        spots.append(tuple(where))
    return values.at[spots[0]].set(least).at[spots[1]].set(largest)


def block_levels(key, shape, cuts, least, top_value):
    loudness = 1.0
    for axis_at, shards_of in cuts:
        steps = jax.random.uniform(jax.random.fold_in(jax.random.fold_in(key, 6), axis_at), (shards_of,), jnp.float32, least / len(cuts), top_value / len(cuts))
        loudness = loudness * jnp.repeat(jnp.exp(steps), shape[axis_at] // shards_of).reshape((-1,) + (1,) * (len(shape) - 1 - axis_at))
    return loudness


def scatter_about(stream_key, shape, scale, bound, shards=(), held_as=jnp.bfloat16):
    array = scale * jax.random.normal(stream_key, shape, jnp.float32)
    if shards:
        array = array * block_levels(stream_key, shape, shards, -0.22, 0.18)
    return jnp.clip(array, -bound, bound).astype(held_as)


def setup_inputs(seed: int = 0) -> dict:
    arg_keys = jax.random.split(jax.random.key(seed), 8)
    amplitudes = scatter_about(arg_keys[0], (NPAIR, NV, NV), 1.0, 6.0, ((0, 32), (1, 8)))
    amp_mask = set_ends((jax.random.randint(arg_keys[1], (NPAIR, NT, NT), 0, 4) < 3).astype(jnp.int32), jax.random.fold_in(arg_keys[1], 1), 0, 1)
    bare_ints = scatter_about(arg_keys[2], (NPAIR, NV, NV), 1.0, 6.0, ((0, 32), (1, 8)))
    int_tiles = scatter_about(arg_keys[3], (N_BLK, N_OWN, OWN_CAP, TILE, TILE), ((LIVE * N_BLK // NT) * TILE) ** -0.5, 0.125, ((0, 8), (1, 32)))
    tile_ids = draw_tile_ids(jax.random.fold_in(arg_keys[7], 71), 0)
    eps_virt = jnp.clip(jax.random.uniform(arg_keys[5], (NV,), jnp.float32, 0.5, 3.0), 0.5, 3.0)
    eps_pair = jnp.clip(-2.0 + 1.5 * jax.random.uniform(arg_keys[6], (NPAIR,), jnp.float32) ** block_levels(arg_keys[6], (NPAIR,), ((0, 32),), -0.2, 0.2), -2.0, -0.5)
    return dict(amplitudes=amplitudes, amp_mask=amp_mask, bare_ints=bare_ints, int_tiles=int_tiles, tile_ids=tile_ids, eps_virt=eps_virt, eps_pair=eps_pair)


def reference(amplitudes, amp_mask, bare_ints, int_tiles, tile_ids, eps_virt, eps_pair):
    row_tiles = NT // N_BLK
    flat_ids = tile_ids.reshape(N_BLK, -1)
    block = jnp.arange(N_BLK, dtype=jnp.int32)[:, None]
    position = jnp.where(flat_ids >= 0, block * (row_tiles * NT) + flat_ids, NT * NT).astype(jnp.int32).reshape(-1)
    tiles = int_tiles.reshape(-1, TILE, TILE).astype(jnp.float32)
    grid = jnp.zeros((NT * NT, TILE, TILE), jnp.float32).at[position].add(tiles, mode="drop")
    wmat = grid.reshape(NT, NT, TILE, TILE).transpose(0, 2, 1, 3).reshape(NT * TILE, NT * TILE)

    def one_pair(items):
        amps, mask, bare, pair_energy = items
        mask_el = jnp.repeat(jnp.repeat(mask, TILE, axis=0), TILE, axis=1).astype(jnp.float32)
        screened = amps.astype(jnp.float32) * mask_el
        cycle = jnp.dot(wmat, screened, precision=lax.Precision.HIGHEST)
        denom = eps_virt[:, None] + eps_virt[None, :] - pair_energy
        return (((bare.astype(jnp.float32) + cycle) / denom) * mask_el).astype(jnp.bfloat16)

    return lax.map(one_pair, (amplitudes, amp_mask, bare_ints, eps_pair))
```

```python
import jax
import jax.numpy as jnp
from jax import lax
from jax.experimental import pallas as pl
from jax.experimental.pallas import tpu as pltpu
from jax.sharding import PartitionSpec as P

TILE = 128
NT = 24
SLOTS = 10
ROWS = 384
NV = 3072
HALF = 1536
NC = 6
CW = HALF // NC
CR = 192
ZC = 384
MESH = pl.DeviceIdType.MESH
BF = jnp.bfloat16
F32 = jnp.float32


def al(value, multiple=128):
    return pl.multiple_of(value, multiple)


def kernel(amp, mask, bare, tiles, ids, eps, pair, out,
           amps, sfull, ssend, barep, bareo, grid, gr, zr, xsend, xr, wf, op, oo, rowe,
           loc, sx, rx, sy, ry, sf, rf, sb, rb, so, ro, lo, sc, rc, sz, rz, sw, rw, sa, ra, sd, rd):
    own, blk = lax.axis_index("own"), lax.axis_index("blk")
    core, z, xl = own % 2, (own // 2) % 8, own // 16
    xh, y = blk // 4, blk % 4

    def dev(xh_=None, y_=None, xl_=None, z_=None, core_=None):
        xh_ = xh if xh_ is None else xh_
        y_ = y if y_ is None else y_
        xl_ = xl if xl_ is None else xl_
        z_ = z if z_ is None else z_
        core_ = core if core_ is None else core_
        return {"own": xl_ * 16 + z_ * 2 + core_, "blk": xh_ * 4 + y_}

    def remote(src, dst, send, recv, device):
        return pltpu.make_async_remote_copy(
            src_ref=src, dst_ref=dst, send_sem=send, recv_sem=recv,
            device_id=device, device_id_type=MESH)

    other = dev(xh_=1 - xh)
    sibling = dev(core_=1 - core)
    yn = [dev(y_=(y + 1) % 4), dev(y_=(y + 3) % 4)]
    zn = [dev(z_=(z + 1) % 8), dev(z_=(z + 7) % 8)]
    zk = [dev(z_=(z + k) % 8) for k in range(1, 8)]
    xs = [dev(xl_=1 - xl), other, dev(xh_=1 - xh, xl_=1 - xl)]

    mine, theirs = al(xh * HALF), al((1 - xh) * HALF)
    load_theirs = pltpu.make_async_copy(amp.at[:, pl.ds(theirs, HALF)], amps.at[:, pl.ds(0, HALF)], loc.at[0])
    load_mine = pltpu.make_async_copy(amp.at[:, pl.ds(mine, HALF)], amps.at[:, pl.ds(HALF, HALF)], loc.at[1])
    load_bare = pltpu.make_async_copy(bare.at[:, pl.ds(mine, HALF)], bareo, loc.at[2])
    load_theirs.start()
    load_mine.start()
    load_bare.start()

    barrier = pltpu.get_barrier_semaphore()
    peers = [sibling] + yn + zk + xs
    for peer in peers:
        pl.semaphore_signal(barrier, inc=1, device_id=peer, device_id_type=MESH)
    pl.semaphore_wait(barrier, len(peers))

    def rows_of(xh_, y_):
        return pl.ds(al((xh_ * 4 + y_) * ROWS), ROWS)

    def cols(n):
        return pl.ds(al(n * CW), CW)

    def x_copy(n):
        return remote(ssend.at[:, cols(n)], sfull.at[rows_of(xh, y), cols(n)], sx.at[n], rx.at[n], other)

    def y_copy(part, d, n):
        where = sfull.at[rows_of(xh if part == 0 else 1 - xh, y), cols(n)]
        return remote(where, where, sy.at[part, d, n], ry.at[part, d, n], yn[d])

    def f_copy(d, n):
        where = sfull.at[rows_of(xh if d == 0 else 1 - xh, (y + 3) % 4 if d == 0 else (y + 1) % 4), cols(n)]
        return remote(where, where, sf.at[d, n], rf.at[d, n], yn[d])

    def b_copy(n):
        return remote(bare.at[:, pl.ds(al(theirs + n * CW), CW)], barep.at[:, cols(n)], sb.at[n], rb.at[n], other)

    def o_copy(n):
        return remote(op.at[:, cols(n)], out.at[:, pl.ds(al(mine + n * CW), CW)], so.at[n], ro.at[n], other)

    def own_out(n):
        return pltpu.make_async_copy(oo.at[:, cols(n)], out.at[:, pl.ds(al(mine + n * CW), CW)], lo.at[n])

    load_theirs.wait()
    load_mine.wait()

    def screen(n, _):
        for side in range(2):
            first = (1 - xh) if side == 0 else xh
            for r in range(3):
                for c in range(CW // TILE):
                    keep = mask[r, first * (NT // 2) + n * (CW // TILE) + c]
                    here = al(n * CW + c * TILE)
                    tile = amps[r * TILE:(r + 1) * TILE, pl.ds(al(side * HALF + here), TILE)]
                    tile = jnp.where(keep > 0, tile, jnp.zeros_like(tile))
                    if side == 0:
                        ssend[r * TILE:(r + 1) * TILE, pl.ds(here, TILE)] = tile
                    else:
                        sfull[pl.ds(al(blk * ROWS + r * TILE), TILE), pl.ds(here, TILE)] = tile
            if side == 0:
                x_copy(n).start()
        y_copy(0, 0, n).start()
        y_copy(0, 1, n).start()
        return 0

    lax.fori_loop(0, NC, screen, 0)

    def place(q, _):
        index, found = 0, 0
        for s in range(SLOTS):
            hit = ids[s] == q
            index = jnp.where(hit, s, index)
            found = jnp.where(hit, 1, found)
        tile = tiles[index]
        grid[pl.ds(al(q // NT * TILE), TILE), pl.ds(al(q % NT * TILE), TILE)] = jnp.where(
            found > 0, tile, jnp.zeros_like(tile))
        return 0

    lax.fori_loop(0, 3 * NT, place, 0)
    half_rows = pl.ds(al(core * CR, 16), CR)
    c_copy = remote(grid.at[pl.ds(al((1 - core) * CR, 16), CR), :], gr, sc, rc, sibling)
    c_copy.start()

    for side in range(2):
        for r in range(3):
            line = eps[pl.ds((side * 4 + y) * 3 + r, 1), :]
            rowe[side, r] = jnp.transpose(jnp.broadcast_to(line, (TILE, TILE)))

    c_copy.wait_recv()

    def add_core(k, _):
        at = pl.ds(al(k * ZC), ZC)
        grid[half_rows, at] = grid[half_rows, at] + gr[:, at]
        return 0

    lax.fori_loop(0, 8, add_core, 0)

    def z_copy(k):
        return remote(grid.at[half_rows, pl.ds(al((z + k) % 8 * ZC), ZC)], zr.at[k - 1], sz.at[k - 1], rz.at[k - 1], zk[k - 1])

    for k in (1, 7, 2, 6, 3, 5, 4):
        z_copy(k).start()

    def spread(n, _):
        x_copy(n).wait_recv()
        y_copy(1, 0, n).start()
        y_copy(1, 1, n).start()
        y_copy(0, 0, n).wait_recv()
        f_copy(0, n).start()
        return 0

    lax.fori_loop(0, NC, spread, 0)
    for n in range(2):
        b_copy(n).start()

    for k in range(1, 8):
        z_copy(k).wait_recv()
    total = grid[half_rows, pl.ds(al(z * ZC), ZC)]
    for k in range(7):
        total = total + zr[k]
    xsend[...] = total
    w_copies = [remote(xsend, xr.at[k], sw.at[k], rw.at[k], xs[k]) for k in range(3)]
    for copy in w_copies:
        copy.start()
    for n in range(2, NC):
        b_copy(n).start()

    def piece(z_, side=None):
        first = slice(None) if side is None else side
        return wf.at[first, half_rows, pl.ds(al(z_ * ZC), ZC)]

    def a_copy(d, s):
        z_ = (z + 8 - s) % 8 if d == 0 else (z + s) % 8
        where = piece(z_, d if s == 3 else None)
        return remote(where, where, sa.at[d, s], ra.at[d, s], zn[d])

    def d_copy(d, s):
        z_ = (z + 8 - s) % 8 if d == 0 else (z + s) % 8
        where = piece(z_, d if s == 4 else None)
        at = 4 * d + s
        return remote(where, where, sd.at[at], rd.at[at], sibling)

    for copy in w_copies:
        copy.wait_recv()
    here = pl.ds(al(z * ZC), ZC)
    wf[xh, half_rows, here] = xsend[...] + xr[0]
    wf[1 - xh, half_rows, here] = xr[1] + xr[2]
    a_copy(0, 0).start()
    a_copy(1, 0).start()
    d_copy(0, 0).start()

    def partner_on(n):
        y_copy(1, 1, n).wait_recv()
        f_copy(1, n).start()

    for s in range(1, 4):
        partner_on(2 * s - 2)
        partner_on(2 * s - 1)
        for d in range(2):
            a_copy(d, s - 1).wait_recv()
            a_copy(d, s).start()
            d_copy(d, s).start()
    for d in range(2):
        a_copy(d, 3).wait_recv()
        d_copy(d, 4).start()
    load_bare.wait()
    d_copy(0, 0).wait_recv()
    for s in range(1, 5):
        for d in range(2):
            d_copy(d, s).wait_recv()

    energy = pair[0]

    def work(n, _):
        y_copy(0, 1, n).wait_recv()
        y_copy(1, 0, n).wait_recv()
        f_copy(0, n).wait_recv()
        f_copy(1, n).wait_recv()
        b_copy(n).wait_recv()
        for which in range(2):
            side = (1 - xh) if which == 0 else xh
            source, target = (barep, op) if which == 0 else (bareo, oo)
            total = jnp.dot(wf[side], sfull[:, cols(n)], preferred_element_type=F32)
            for r in range(3):
                for c in range(CW // TILE):
                    at = pl.ds(al(n * CW + c * TILE), TILE)
                    line = eps[pl.ds(xh * (NT // 2) + n * (CW // TILE) + c, 1), :]
                    denom = (rowe[side, r] + line) - energy
                    value = source[r * TILE:(r + 1) * TILE, at].astype(F32) + total[r * TILE:(r + 1) * TILE, c * TILE:(c + 1) * TILE]
                    target[r * TILE:(r + 1) * TILE, at] = (value / denom).astype(BF)
            if which == 0:
                o_copy(n).start()
            else:
                own_out(n).start()
        return 0

    lax.fori_loop(0, NC, work, 0)

    def drain(n, _):
        own_out(n).wait()
        x_copy(n).wait_send()
        b_copy(n).wait_send()
        for d in range(2):
            y_copy(0, d, n).wait_send()
            y_copy(1, d, n).wait_send()
            f_copy(d, n).wait_send()
        o_copy(n).wait_send()
        o_copy(n).wait_recv()
        return 0

    lax.fori_loop(0, NC, drain, 0)
    c_copy.wait_send()
    for k in range(1, 8):
        z_copy(k).wait_send()
    for copy in w_copies:
        copy.wait_send()
    d_copy(0, 0).wait_send()
    for d in range(2):
        for s in range(4):
            a_copy(d, s).wait_send()
            d_copy(d, s + 1).wait_send()


def apply_mask(mask, raw, out):
    for r in range(3):
        for c in range(NT):
            at = (slice(r * TILE, (r + 1) * TILE), slice(c * TILE, (c + 1) * TILE))
            tile = raw[at]
            out[at] = jnp.where(mask[r, c] > 0, tile, jnp.zeros_like(tile))


def local(amplitudes, amp_mask, bare_ints, int_tiles, tile_ids, eps_virt, eps_pair):
    dma = pltpu.SemaphoreType.DMA
    vmem = pltpu.VMEM
    mask = amp_mask.reshape(3, NT)
    anywhere = pl.BlockSpec(memory_space=pl.ANY)
    smem = pl.BlockSpec(memory_space=pltpu.SMEM)
    inside = pl.BlockSpec(memory_space=pltpu.VMEM)
    pairs_of = [dma((NC,)), dma((NC,)), dma((2, 2, NC)), dma((2, 2, NC)), dma((2, NC)), dma((2, NC)),
                dma((NC,)), dma((NC,)), dma((NC,)), dma((NC,)), dma((NC,)),
                dma, dma, dma((7,)), dma((7,)), dma((3,)), dma((3,)),
                dma((2, 4)), dma((2, 4)), dma((9,)), dma((9,))]
    raw = pl.pallas_call(
        kernel,
        out_shape=jax.ShapeDtypeStruct((ROWS, NV), BF),
        in_specs=[anywhere, smem, anywhere, inside, smem, inside, smem],
        out_specs=anywhere,
        scratch_shapes=[
            vmem((ROWS, NV), BF), vmem((NV, HALF), BF), vmem((ROWS, HALF), BF), vmem((ROWS, HALF), BF),
            vmem((ROWS, HALF), BF), vmem((ROWS, NV), BF), vmem((CR, NV), BF), vmem((7, CR, ZC), BF),
            vmem((CR, ZC), BF), vmem((3, CR, ZC), BF), vmem((2, ROWS, NV), BF), vmem((ROWS, HALF), BF),
            vmem((ROWS, HALF), BF), vmem((2, 3, TILE, TILE), F32),
            dma((3,)), *pairs_of,
        ],
        compiler_params=pltpu.CompilerParams(
            collective_id=0, has_side_effects=True, vmem_limit_bytes=56 * 1024 * 1024),
        name="cycle",
    )(amplitudes.reshape(ROWS, NV), mask, bare_ints.reshape(ROWS, NV), int_tiles.reshape(SLOTS, TILE, TILE),
      tile_ids.reshape(SLOTS), eps_virt.reshape(NT, TILE), eps_pair)
    final = pl.pallas_call(
        apply_mask,
        out_shape=jax.ShapeDtypeStruct((ROWS, NV), BF),
        in_specs=[smem, inside],
        out_specs=inside,
        name="screen",
    )(mask, raw)
    return final.reshape(1, ROWS, NV)


def solution(mesh):
    in_specs = (
        P("own", "blk", None),
        P("own", "blk", None),
        P("own", "blk", None),
        P("blk", "own", None, None, None),
        P("blk", "own", None),
        P(),
        P("own"),
    )
    return jax.shard_map(local, mesh=mesh, in_specs=in_specs, out_specs=P("own", "blk", None), check_vma=False)
```

```python
import jax
import jax.numpy as jnp
from jax import lax
from jax.experimental import pallas as pl
from jax.experimental.pallas import tpu as pltpu
from jax.sharding import PartitionSpec as P

TILE = 128
NT = 24
SLOTS = 10
ROWS = 384
NV = 3072
HALF = 1536
QR = 32
ZC = 384
STARTS = (0, 256, 512, 768, 1024, 1280, 1408)
WIDTHS = (256, 256, 256, 256, 256, 128, 128)
NC = len(STARTS)
WIDE = 256
MESH = pl.DeviceIdType.MESH
BF = jnp.bfloat16
F32 = jnp.float32


def al(value, multiple=128):
    return pl.multiple_of(value, multiple)


def kernel(amp, mask, bare, tiles, ids, eps, pair, out,
           amps, sfull, ssend, barep, bareo, inv, tr, grid, zr, xsend, xr, wf, op, oo, rowe, mv,
           loc, sx, rx, sy, ry, sf, rf, sb, rb, so, ro, lo, sm, rm, si, ri, st, rt, sz, rz, sw, rw, sa, ra, sd, rd):
    own, blk = lax.axis_index("own"), lax.axis_index("blk")
    core, z, xl = own % 2, (own // 2) % 8, own // 16
    xh, y = blk // 4, blk % 4

    def dev(xh_=None, y_=None, xl_=None, z_=None, core_=None):
        xh_ = xh if xh_ is None else xh_
        y_ = y if y_ is None else y_
        xl_ = xl if xl_ is None else xl_
        z_ = z if z_ is None else z_
        core_ = core if core_ is None else core_
        return {"own": xl_ * 16 + z_ * 2 + core_, "blk": xh_ * 4 + y_}

    def remote(src, dst, send, recv, device):
        return pltpu.make_async_remote_copy(
            src_ref=src, dst_ref=dst, send_sem=send, recv_sem=recv,
            device_id=device, device_id_type=MESH)

    other = dev(xh_=1 - xh)
    sibling = dev(core_=1 - core)
    yn = [dev(y_=(y + 1) % 4), dev(y_=(y + 3) % 4)]
    zk = [dev(z_=(z + k) % 8) for k in range(1, 8)]
    zn = [zk[0], zk[6]]
    xs = [dev(xl_=1 - xl), other, dev(xh_=1 - xh, xl_=1 - xl)]
    quad = [sibling, dev(xl_=1 - xl), dev(xl_=1 - xl, core_=1 - core)]
    quarter = core * 2 + xl
    quarters = [(1 - core) * 2 + xl, core * 2 + 1 - xl, (1 - core) * 2 + 1 - xl]

    mine, theirs = al(xh * HALF), al((1 - xh) * HALF)
    load_theirs = pltpu.make_async_copy(amp.at[:, pl.ds(theirs, HALF)], amps.at[:, pl.ds(0, HALF)], loc.at[0])
    load_mine = pltpu.make_async_copy(amp.at[:, pl.ds(mine, HALF)], amps.at[:, pl.ds(HALF, HALF)], loc.at[1])
    load_bare = pltpu.make_async_copy(bare.at[:, pl.ds(mine, HALF)], bareo, loc.at[2])
    load_theirs.start()
    load_mine.start()
    load_bare.start()

    barrier = pltpu.get_barrier_semaphore()
    peers = yn + zk + xs + [sibling, quad[2]]
    for peer in peers:
        pl.semaphore_signal(barrier, inc=1, device_id=peer, device_id_type=MESH)

    def invert(q, _):
        slot = SLOTS
        for s in range(SLOTS):
            slot = jnp.where(ids[s] == q, s, slot)
        inv[0, q] = slot
        return 0

    lax.fori_loop(0, 3 * NT, invert, 0)
    pl.semaphore_wait(barrier, len(peers))

    def rows_of(xh_, y_):
        return pl.ds(al((xh_ * 4 + y_) * ROWS), ROWS)

    def part(n, base=0):
        if isinstance(n, int):
            return pl.ds(al(base + STARTS[n]), WIDTHS[n])
        return pl.ds(al(base + n * WIDE), WIDE)

    def x_copy(n):
        return remote(ssend.at[:, part(n)], sfull.at[rows_of(xh, y), part(n)], sx.at[n], rx.at[n], other)

    def y_copy(b, d, n):
        where = sfull.at[rows_of(xh if b == 0 else 1 - xh, y), part(n)]
        return remote(where, where, sy.at[b, d, n], ry.at[b, d, n], yn[d])

    def f_copy(d, n):
        where = sfull.at[rows_of(xh if d == 0 else 1 - xh, (y + 3) % 4 if d == 0 else (y + 1) % 4), part(n)]
        return remote(where, where, sf.at[d, n], rf.at[d, n], yn[d])

    def b_copy(n):
        return remote(bare.at[:, part(n, theirs)], barep.at[:, part(n)], sb.at[n], rb.at[n], other)

    def o_copy(n):
        return remote(op.at[:, part(n)], out.at[:, part(n, mine)], so.at[n], ro.at[n], other)

    def own_out(n):
        at = n * WIDE
        return pltpu.make_async_copy(oo.at[:, pl.ds(al(at), WIDE)], out.at[:, pl.ds(al(mine + at), WIDE)], lo.at[n])

    def t_copy(j):
        return remote(tiles.at[:, pl.ds(al(quarters[j] * QR, QR), QR), :], tr.at[j + 1, pl.ds(0, SLOTS)], st.at[j], rt.at[j], quad[j])

    def i_copy(j):
        return remote(inv.at[0], inv.at[j + 1], si.at[j], ri.at[j], quad[j])

    for j in range(3):
        t_copy(j).start()
        i_copy(j).start()

    def screen(n):
        count = WIDTHS[n] // TILE
        for side in range(2):
            first = (1 - xh) if side == 0 else xh
            for c in range(count):
                here = STARTS[n] + c * TILE
                for r in range(3):
                    keep = mask[r, 0, first * (NT // 2) + here // TILE]
                    tile = amps[r * TILE:(r + 1) * TILE, side * HALF + here:side * HALF + here + TILE]
                    tile = jnp.where(keep > 0, tile, jnp.zeros_like(tile))
                    if side == 0:
                        ssend[r * TILE:(r + 1) * TILE, here:here + TILE] = tile
                    else:
                        sfull[pl.ds(al(blk * ROWS + r * TILE), TILE), here:here + TILE] = tile
            if side == 0:
                x_copy(n).start()
        y_copy(0, 0, n).start()
        y_copy(0, 1, n).start()

    load_theirs.wait()
    load_mine.wait()
    screen(0)
    screen(1)

    for s in range(SLOTS):
        tr[0, s] = tiles[s, pl.ds(al(quarter * QR, QR), QR), :]
    for j in range(4):
        tr[j, SLOTS] = jnp.zeros((QR, TILE), BF)
    for j in range(3):
        t_copy(j).wait_recv()
        i_copy(j).wait_recv()

    def place(q, _):
        tile = tr[0, inv[0, q]]
        for j in range(1, 4):
            tile = tile + tr[j, inv[j, q]]
        grid[pl.ds(al(q // NT * QR, QR), QR), pl.ds(al(q % NT * TILE), TILE)] = tile
        return 0

    lax.fori_loop(0, 3 * NT, place, 0)
    here = pl.ds(al(z * ZC), ZC)

    def z_copy(k):
        return remote(grid.at[:, pl.ds(al((z + k) % 8 * ZC), ZC)], zr.at[k - 1], sz.at[k - 1], rz.at[k - 1], zk[k - 1])

    for k in (4, 3, 5, 2, 6, 1, 7):
        z_copy(k).start()

    for n in range(2, NC):
        screen(n)

    def spread_mask(c, _):
        for r in range(3):
            mv[1, r, pl.ds(c, 1), :] = jnp.full((1, TILE), mask[r, 0, c].astype(F32))
        return 0

    lax.fori_loop(0, NT, spread_mask, 0)
    m_copy = remote(mv.at[1], mv.at[0], sm, rm, other)
    m_copy.start()

    for side in range(2):
        for r in range(3):
            line = eps[pl.ds((side * 4 + y) * 3 + r, 1), :]
            rowe[side, r] = jnp.transpose(jnp.broadcast_to(line, (TILE, TILE)))

    def spread(n):
        x_copy(n).wait_recv()
        y_copy(1, 0, n).start()
        y_copy(1, 1, n).start()
        y_copy(0, 0, n).wait_recv()
        f_copy(0, n).start()

    def partner_on(n):
        y_copy(1, 1, n).wait_recv()
        f_copy(1, n).start()

    def w_copy(k):
        return remote(xsend, xr.at[k], sw.at[k], rw.at[k], xs[k])

    def reduce_z():
        for k in range(1, 8):
            z_copy(k).wait_recv()
        total = grid[:, here]
        for k in range(7):
            total = total + zr[k]
        xsend[...] = total
        for k in range(3):
            w_copy(k).start()

    def reduce_x():
        for k in range(3):
            w_copy(k).wait_recv()
        for r in range(3):
            rows = slice(r * QR, (r + 1) * QR)
            wf[xh, r, quarter, :, here] = xsend[rows, :]
            wf[xh, r, quarters[1], :, here] = xr[0, rows, :]
            wf[1 - xh, r, quarter, :, here] = xr[1, rows, :]
            wf[1 - xh, r, quarters[1], :, here] = xr[2, rows, :]

    def piece(g, z_, q=None):
        which = pl.ds(core * 2, 2) if q is None else pl.ds(core * 2 + q, 1)
        return wf.at[1 - xh if g == 0 else xh, :, which, :, pl.ds(al(z_ * ZC), ZC)]

    def from_z(d, s):
        return (z + 8 - s) % 8 if d == 0 else (z + s) % 8

    def a_copy(g, d, s):
        where = piece(g, from_z(d, s), d if s == 3 else None)
        return remote(where, where, sa.at[g, d, s], ra.at[g, d, s], zn[d])

    def d_copy(g, d, s):
        where = piece(g, from_z(d, s), d if s == 4 else None)
        return remote(where, where, sd.at[g, 4 * d + s], rd.at[g, 4 * d + s], sibling)

    def begin(g):
        a_copy(g, 0, 0).start()
        a_copy(g, 1, 0).start()
        d_copy(g, 0, 0).start()

    def onward(g, s):
        for d in range(2):
            a_copy(g, d, s - 1).wait_recv()
            if s < 4:
                a_copy(g, d, s).start()
            d_copy(g, d, s).start()

    def gathered(g):
        d_copy(g, 0, 0).wait_recv()
        for s in range(1, 5):
            for d in range(2):
                d_copy(g, d, s).wait_recv()

    for n in range(4):
        spread(n)
    reduce_z()
    spread(4)
    spread(5)
    spread(6)
    reduce_x()
    begin(0)
    begin(1)
    for n in range(NC):
        b_copy(n).start()
    onward(0, 1)
    onward(1, 1)
    onward(0, 2)
    partner_on(0)
    onward(1, 2)
    partner_on(1)
    onward(0, 3)
    partner_on(2)
    onward(1, 3)
    onward(0, 4)
    partner_on(3)
    onward(1, 4)
    partner_on(4)
    partner_on(5)
    partner_on(6)
    load_bare.wait()
    m_copy.wait_recv()
    gathered(0)
    gathered(1)

    energy = pair[0]

    def rows_done(start, width, which):
        side = (1 - xh) if which == 0 else xh
        source, target = (barep, op) if which == 0 else (bareo, oo)
        total = jnp.dot(wf[side].reshape(ROWS, NV), sfull[:, pl.ds(al(start), width)], preferred_element_type=F32)
        for c in range(width // TILE):
            at = pl.ds(al(start + c * TILE), TILE)
            column = xh * (NT // 2) + start // TILE + c
            line = eps[pl.ds(column, 1), :]
            for r in range(3):
                rows = slice(r * TILE, (r + 1) * TILE)
                denom = (rowe[side, r] + line) - energy
                value = source[rows, at].astype(F32) + total[rows, c * TILE:(c + 1) * TILE]
                target[rows, at] = (value / denom * mv[which, r, pl.ds(column, 1), :]).astype(BF)

    def theirs_done(n, start, width):
        y_copy(0, 1, n).wait_recv()
        y_copy(1, 0, n).wait_recv()
        f_copy(0, n).wait_recv()
        f_copy(1, n).wait_recv()
        b_copy(n).wait_recv()
        rows_done(start, width, 0)
        o_copy(n).start()

    def mine_done(n):
        rows_done(n * WIDE, WIDE, 1)
        own_out(n).start()

    theirs_done(0, 0, WIDE)

    def work(n, _):
        theirs_done(n, n * WIDE, WIDE)
        mine_done(n - 1)
        return 0

    lax.fori_loop(1, 5, work, 0)
    theirs_done(5, STARTS[5], WIDTHS[5])
    mine_done(4)
    theirs_done(6, STARTS[6], WIDTHS[6])
    mine_done(5)

    for n in range(6):
        own_out(n).wait()
    for j in range(3):
        t_copy(j).wait_send()
        i_copy(j).wait_send()
    m_copy.wait_send()
    for n in range(NC):
        x_copy(n).wait_send()
        b_copy(n).wait_send()
        for d in range(2):
            y_copy(0, d, n).wait_send()
            y_copy(1, d, n).wait_send()
            f_copy(d, n).wait_send()
    for k in range(1, 8):
        z_copy(k).wait_send()
    for k in range(3):
        w_copy(k).wait_send()
    for g in range(2):
        d_copy(g, 0, 0).wait_send()
        for d in range(2):
            for t in range(4):
                a_copy(g, d, t).wait_send()
                d_copy(g, d, t + 1).wait_send()
    for n in range(NC):
        o_copy(n).wait_send()
        o_copy(n).wait_recv()


def local(amplitudes, amp_mask, bare_ints, int_tiles, tile_ids, eps_virt, eps_pair):
    dma = pltpu.SemaphoreType.DMA
    vmem = pltpu.VMEM
    anywhere = pl.BlockSpec(memory_space=pl.ANY)
    smem = pl.BlockSpec(memory_space=pltpu.SMEM)
    inside = pl.BlockSpec(memory_space=pltpu.VMEM)
    sizes = [(NC,), (2, 2, NC), (2, NC), (NC,), (NC,)]
    sems = [dma(size) for size in sizes for _ in range(2)] + [dma((6,)), dma, dma]
    sems += [dma(size) for size in [(3,), (3,), (7,), (3,), (2, 2, 4), (2, 9)] for _ in range(2)]
    result = pl.pallas_call(
        kernel,
        out_shape=jax.ShapeDtypeStruct((ROWS, NV), BF),
        in_specs=[anywhere, smem, anywhere, inside, smem, inside, smem],
        out_specs=anywhere,
        scratch_shapes=[
            vmem((ROWS, NV), BF), vmem((NV, HALF), BF), vmem((ROWS, HALF), BF), vmem((ROWS, HALF), BF),
            vmem((ROWS, HALF), BF), pltpu.SMEM((4, TILE), jnp.int32), vmem((4, SLOTS + 1, QR, TILE), BF),
            vmem((3 * QR, NV), BF), vmem((7, 3 * QR, ZC), BF), vmem((3 * QR, ZC), BF), vmem((3, 3 * QR, ZC), BF),
            vmem((2, 3, 4, QR, NV), BF), vmem((ROWS, HALF), BF), vmem((ROWS, HALF), BF),
            vmem((2, 3, TILE, TILE), F32), vmem((2, 3, NT, TILE), F32),
            dma((3,)), *sems,
        ],
        compiler_params=pltpu.CompilerParams(
            collective_id=0, has_side_effects=True, vmem_limit_bytes=56 * 1024 * 1024),
        name="cycle",
    )(amplitudes.reshape(ROWS, NV), amp_mask.reshape(3, 1, NT), bare_ints.reshape(ROWS, NV),
      int_tiles.reshape(SLOTS, TILE, TILE), tile_ids.reshape(SLOTS), eps_virt.reshape(NT, TILE), eps_pair)
    return result.reshape(1, ROWS, NV)


def solution(mesh):
    in_specs = (
        P("own", "blk", None),
        P("own", "blk", None),
        P("own", "blk", None),
        P("blk", "own", None, None, None),
        P("blk", "own", None),
        P(),
        P("own"),
    )
    return jax.shard_map(local, mesh=mesh, in_specs=in_specs, out_specs=P("own", "blk", None), check_vma=False)
```

```python
import jax
import jax.numpy as jnp
from jax import lax
from jax.experimental import pallas as pl
from jax.experimental.pallas import tpu as pltpu
from jax.sharding import PartitionSpec as P

TILE = 128
NT = 24
SLOTS = 10
ROWS = 384
NV = 3072
HALF = 1536
QR = 32
ZC = 384
STARTS = (0, 256, 512, 768, 1024, 1280, 1408)
WIDTHS = (256, 256, 256, 256, 256, 128, 128)
NC = len(STARTS)
WIDE = 256
MESH = pl.DeviceIdType.MESH
BF = jnp.bfloat16
F32 = jnp.float32


def al(value, multiple=128):
    return pl.multiple_of(value, multiple)


def kernel(amp, mask, bare, tiles, ids, eps, pair, out,
           amps, sfull, ssend, barep, bareo, inv, tr, grid, zr, xsend, xr, wf, op, rowe, mv,
           loc, sx, rx, sy, ry, sf, rf, sb, rb, so, ro, sm, rm, si, ri, st, rt, sz, rz, sw, rw, sa, ra, sd, rd):
    own, blk = lax.axis_index("own"), lax.axis_index("blk")
    core, z, xl = own % 2, (own // 2) % 8, own // 16
    xh, y = blk // 4, blk % 4

    def dev(xh_=None, y_=None, xl_=None, z_=None, core_=None):
        xh_ = xh if xh_ is None else xh_
        y_ = y if y_ is None else y_
        xl_ = xl if xl_ is None else xl_
        z_ = z if z_ is None else z_
        core_ = core if core_ is None else core_
        return {"own": xl_ * 16 + z_ * 2 + core_, "blk": xh_ * 4 + y_}

    def remote(src, dst, send, recv, device):
        return pltpu.make_async_remote_copy(
            src_ref=src, dst_ref=dst, send_sem=send, recv_sem=recv,
            device_id=device, device_id_type=MESH)

    other = dev(xh_=1 - xh)
    sibling = dev(core_=1 - core)
    yn = [dev(y_=(y + 1) % 4), dev(y_=(y + 3) % 4)]
    zk = [dev(z_=(z + k) % 8) for k in range(1, 8)]
    zn = [zk[0], zk[6]]
    xs = [dev(xl_=1 - xl), other, dev(xh_=1 - xh, xl_=1 - xl)]
    quad = [sibling, dev(xl_=1 - xl), dev(xl_=1 - xl, core_=1 - core)]
    quarter = core * 2 + xl
    quarters = [(1 - core) * 2 + xl, core * 2 + 1 - xl, (1 - core) * 2 + 1 - xl]

    mine, theirs = al(xh * HALF), al((1 - xh) * HALF)
    load_theirs = pltpu.make_async_copy(amp.at[:, pl.ds(theirs, HALF)], amps.at[:, pl.ds(0, HALF)], loc.at[0])
    load_mine = pltpu.make_async_copy(amp.at[:, pl.ds(mine, HALF)], amps.at[:, pl.ds(HALF, HALF)], loc.at[1])
    load_bare = pltpu.make_async_copy(bare.at[:, pl.ds(mine, HALF)], bareo, loc.at[2])
    load_theirs.start()
    load_mine.start()
    load_bare.start()

    barrier = pltpu.get_barrier_semaphore()
    peers = yn + zk + xs + [sibling, quad[2]]
    for peer in peers:
        pl.semaphore_signal(barrier, inc=1, device_id=peer, device_id_type=MESH)

    def invert(q, _):
        slot = SLOTS
        for s in range(SLOTS):
            slot = jnp.where(ids[s] == q, s, slot)
        inv[0, q] = slot
        return 0

    lax.fori_loop(0, 3 * NT, invert, 0)
    pl.semaphore_wait(barrier, len(peers))

    def rows_of(xh_, y_):
        return pl.ds(al((xh_ * 4 + y_) * ROWS), ROWS)

    def part(n, base=0):
        if isinstance(n, int):
            return pl.ds(al(base + STARTS[n]), WIDTHS[n])
        return pl.ds(al(base + n * WIDE), WIDE)

    def x_copy(n):
        return remote(ssend.at[:, part(n)], sfull.at[rows_of(xh, y), part(n)], sx.at[n], rx.at[n], other)

    def y_copy(b, d, n):
        where = sfull.at[rows_of(xh if b == 0 else 1 - xh, y), part(n)]
        return remote(where, where, sy.at[b, d, n], ry.at[b, d, n], yn[d])

    def f_copy(d, n):
        where = sfull.at[rows_of(xh if d == 0 else 1 - xh, (y + 3) % 4 if d == 0 else (y + 1) % 4), part(n)]
        return remote(where, where, sf.at[d, n], rf.at[d, n], yn[d])

    def b_copy(n):
        return remote(bare.at[:, part(n, theirs)], barep.at[:, part(n)], sb.at[n], rb.at[n], other)

    def o_copy(n):
        return remote(op.at[:, part(n)], out.at[:, part(n, mine)], so.at[n], ro.at[n], other)

    def t_copy(j):
        return remote(tiles.at[:, pl.ds(al(quarters[j] * QR, QR), QR), :], tr.at[j + 1, pl.ds(0, SLOTS)], st.at[j], rt.at[j], quad[j])

    def i_copy(j):
        return remote(inv.at[0], inv.at[j + 1], si.at[j], ri.at[j], quad[j])

    for j in range(3):
        t_copy(j).start()
        i_copy(j).start()

    def screen(n, send=True):
        count = WIDTHS[n] // TILE
        for side in range(2):
            first = (1 - xh) if side == 0 else xh
            for c in range(count):
                here = STARTS[n] + c * TILE
                for r in range(3):
                    keep = mask[r, 0, first * (NT // 2) + here // TILE]
                    tile = amps[r * TILE:(r + 1) * TILE, side * HALF + here:side * HALF + here + TILE]
                    tile = jnp.where(keep > 0, tile, jnp.zeros_like(tile))
                    if side == 0:
                        ssend[r * TILE:(r + 1) * TILE, here:here + TILE] = tile
                    else:
                        sfull[pl.ds(al(blk * ROWS + r * TILE), TILE), here:here + TILE] = tile
            if side == 0 and send:
                x_copy(n).start()
        y_copy(0, 0, n).start()
        y_copy(0, 1, n).start()

    load_theirs.wait()
    load_mine.wait()
    for n in range(4):
        screen(n)
    b_copy(0).start()

    for s in range(SLOTS):
        tr[0, s] = tiles[s, pl.ds(al(quarter * QR, QR), QR), :]
    for j in range(4):
        tr[j, SLOTS] = jnp.zeros((QR, TILE), BF)
    for j in range(3):
        t_copy(j).wait_recv()
        i_copy(j).wait_recv()

    def place(q, _):
        tile = tr[0, inv[0, q]]
        for j in range(1, 4):
            tile = tile + tr[j, inv[j, q]]
        grid[pl.ds(al(q // NT * QR, QR), QR), pl.ds(al(q % NT * TILE), TILE)] = tile
        return 0

    lax.fori_loop(0, 3 * NT, place, 0)
    here = pl.ds(al(z * ZC), ZC)

    def z_copy(k):
        return remote(grid.at[:, pl.ds(al((z + k) % 8 * ZC), ZC)], zr.at[k - 1], sz.at[k - 1], rz.at[k - 1], zk[k - 1])

    for k in (4, 3, 5, 2, 6, 1, 7):
        z_copy(k).start()

    for n in range(4, NC):
        screen(n, False)

    def spread_mask(c, _):
        for r in range(3):
            mv[1, r, pl.ds(c, 1), :] = jnp.full((1, TILE), mask[r, 0, c].astype(F32))
        return 0

    lax.fori_loop(0, NT, spread_mask, 0)
    m_copy = remote(mv.at[1], mv.at[0], sm, rm, other)
    m_copy.start()

    for side in range(2):
        for r in range(3):
            line = eps[pl.ds((side * 4 + y) * 3 + r, 1), :]
            rowe[side, r] = jnp.transpose(jnp.broadcast_to(line, (TILE, TILE)))

    def spread(n):
        x_copy(n).wait_recv()
        y_copy(1, 0, n).start()
        y_copy(1, 1, n).start()
        y_copy(0, 0, n).wait_recv()
        f_copy(0, n).start()

    def partner_on(n):
        y_copy(1, 1, n).wait_recv()
        f_copy(1, n).start()

    def w_copy(k):
        return remote(xsend, xr.at[k], sw.at[k], rw.at[k], xs[k])

    def reduce_z():
        for k in range(1, 8):
            z_copy(k).wait_recv()
        total = grid[:, here]
        for k in range(7):
            total = total + zr[k]
        xsend[...] = total
        for k in range(3):
            w_copy(k).start()

    def reduce_x():
        for k in range(3):
            w_copy(k).wait_recv()
        for r in range(3):
            rows = slice(r * QR, (r + 1) * QR)
            wf[xh, r, quarter, :, here] = xsend[rows, :]
            wf[xh, r, quarters[1], :, here] = xr[0, rows, :]
            wf[1 - xh, r, quarter, :, here] = xr[1, rows, :]
            wf[1 - xh, r, quarters[1], :, here] = xr[2, rows, :]

    def piece(g, z_, q=None):
        which = pl.ds(core * 2, 2) if q is None else pl.ds(core * 2 + q, 1)
        return wf.at[1 - xh if g == 0 else xh, :, which, :, pl.ds(al(z_ * ZC), ZC)]

    def from_z(d, s):
        return (z + 8 - s) % 8 if d == 0 else (z + s) % 8

    def a_copy(g, d, s):
        where = piece(g, from_z(d, s), d if s == 3 else None)
        return remote(where, where, sa.at[g, d, s], ra.at[g, d, s], zn[d])

    def d_copy(g, d, s):
        where = piece(g, from_z(d, s), d if s == 4 else None)
        return remote(where, where, sd.at[g, 4 * d + s], rd.at[g, 4 * d + s], sibling)

    def begin(g):
        a_copy(g, 0, 0).start()
        a_copy(g, 1, 0).start()
        d_copy(g, 0, 0).start()

    def onward(g, s):
        for d in range(2):
            a_copy(g, d, s - 1).wait_recv()
            if s < 4:
                a_copy(g, d, s).start()
            d_copy(g, d, s).start()

    def gathered(g):
        d_copy(g, 0, 0).wait_recv()
        for s in range(1, 5):
            for d in range(2):
                d_copy(g, d, s).wait_recv()

    for n in range(3):
        spread(n)
    reduce_z()
    for n in range(4, NC):
        x_copy(n).start()
    for n in range(1, NC):
        b_copy(n).start()
    spread(3)
    reduce_x()
    begin(0)
    spread(4)
    onward(0, 1)
    begin(1)
    spread(5)
    spread(6)
    onward(0, 2)
    onward(1, 1)
    partner_on(0)
    onward(0, 3)
    onward(1, 2)
    partner_on(1)
    partner_on(2)
    onward(0, 4)
    partner_on(3)
    onward(1, 3)
    partner_on(4)
    load_bare.wait()
    m_copy.wait_recv()
    gathered(0)
    onward(1, 4)
    partner_on(5)
    partner_on(6)

    energy = pair[0]

    def rows_done(start, width, which):
        side = (1 - xh) if which == 0 else xh
        source = barep if which == 0 else bareo
        total = jnp.dot(wf[side].reshape(ROWS, NV), sfull[:, pl.ds(al(start), width)], preferred_element_type=F32)
        for c in range(width // TILE):
            at = pl.ds(al(start + c * TILE), TILE)
            column = xh * (NT // 2) + start // TILE + c
            line = eps[pl.ds(column, 1), :]
            for r in range(3):
                rows = slice(r * TILE, (r + 1) * TILE)
                denom = (rowe[side, r] + line) - energy
                value = source[rows, at].astype(F32) + total[rows, c * TILE:(c + 1) * TILE]
                value = (value / denom * mv[which, r, pl.ds(column, 1), :]).astype(BF)
                if which == 0:
                    op[rows, at] = value
                else:
                    out[rows, pl.ds(al(mine + start + c * TILE), TILE)] = value

    def theirs_done(n, start, width):
        y_copy(0, 1, n).wait_recv()
        y_copy(1, 0, n).wait_recv()
        f_copy(0, n).wait_recv()
        f_copy(1, n).wait_recv()
        b_copy(n).wait_recv()
        rows_done(start, width, 0)
        o_copy(n).start()

    def mine_done(n):
        rows_done(n * WIDE, WIDE, 1)

    theirs_done(0, 0, WIDE)
    gathered(1)

    def work(n, _):
        theirs_done(n, n * WIDE, WIDE)
        mine_done(n - 1)
        return 0

    lax.fori_loop(1, 5, work, 0)
    theirs_done(5, STARTS[5], WIDTHS[5])
    mine_done(4)
    theirs_done(6, STARTS[6], WIDTHS[6])
    mine_done(5)

    for j in range(3):
        t_copy(j).wait_send()
        i_copy(j).wait_send()
    m_copy.wait_send()
    for n in range(NC):
        x_copy(n).wait_send()
        b_copy(n).wait_send()
        for d in range(2):
            y_copy(0, d, n).wait_send()
            y_copy(1, d, n).wait_send()
            f_copy(d, n).wait_send()
    for k in range(1, 8):
        z_copy(k).wait_send()
    for k in range(3):
        w_copy(k).wait_send()
    for g in range(2):
        d_copy(g, 0, 0).wait_send()
        for d in range(2):
            for t in range(4):
                a_copy(g, d, t).wait_send()
                d_copy(g, d, t + 1).wait_send()
    for n in range(NC):
        o_copy(n).wait_send()
        o_copy(n).wait_recv()


def local(amplitudes, amp_mask, bare_ints, int_tiles, tile_ids, eps_virt, eps_pair):
    dma = pltpu.SemaphoreType.DMA
    vmem = pltpu.VMEM
    anywhere = pl.BlockSpec(memory_space=pl.ANY)
    smem = pl.BlockSpec(memory_space=pltpu.SMEM)
    inside = pl.BlockSpec(memory_space=pltpu.VMEM)
    sizes = [(NC,), (2, 2, NC), (2, NC), (NC,), (NC,)]
    sems = [dma(size) for size in sizes for _ in range(2)] + [dma, dma]
    sems += [dma(size) for size in [(3,), (3,), (7,), (3,), (2, 2, 4), (2, 9)] for _ in range(2)]
    result = pl.pallas_call(
        kernel,
        out_shape=vmem((ROWS, NV), BF),
        in_specs=[anywhere, smem, anywhere, inside, smem, inside, smem],
        out_specs=inside,
        scratch_shapes=[
            vmem((ROWS, NV), BF), vmem((NV, HALF), BF), vmem((ROWS, HALF), BF), vmem((ROWS, HALF), BF),
            vmem((ROWS, HALF), BF), pltpu.SMEM((4, TILE), jnp.int32), vmem((4, SLOTS + 1, QR, TILE), BF),
            vmem((3 * QR, NV), BF), vmem((7, 3 * QR, ZC), BF), vmem((3 * QR, ZC), BF), vmem((3, 3 * QR, ZC), BF),
            vmem((2, 3, 4, QR, NV), BF), vmem((ROWS, HALF), BF),
            vmem((2, 3, TILE, TILE), F32), vmem((2, 3, NT, TILE), F32),
            dma((3,)), *sems,
        ],
        compiler_params=pltpu.CompilerParams(
            collective_id=0, has_side_effects=True, vmem_limit_bytes=56 * 1024 * 1024),
        name="cycle",
    )(amplitudes.reshape(ROWS, NV), amp_mask.reshape(3, 1, NT), bare_ints.reshape(ROWS, NV),
      int_tiles.reshape(SLOTS, TILE, TILE), tile_ids.reshape(SLOTS), eps_virt.reshape(NT, TILE), eps_pair)
    return result.reshape(1, ROWS, NV)


def solution(mesh):
    in_specs = (
        P("own", "blk", None),
        P("own", "blk", None),
        P("own", "blk", None),
        P("blk", "own", None, None, None),
        P("blk", "own", None),
        P(),
        P("own"),
    )
    return jax.shard_map(local, mesh=mesh, in_specs=in_specs, out_specs=P("own", "blk", None), check_vma=False)
```

```python
import jax
import jax.numpy as jnp
from jax import lax
from jax.experimental import pallas as pl
from jax.experimental.pallas import tpu as pltpu
from jax.sharding import PartitionSpec as P

TILE = 128
NT = 24
SLOTS = 10
ROWS = 384
NV = 3072
HALF = 1536
QR = 32
ZC = 384
STARTS = (0, 256, 512, 768, 1024, 1280, 1408)
WIDTHS = (256, 256, 256, 256, 256, 128, 128)
NC = len(STARTS)
WIDE = 256
MESH = pl.DeviceIdType.MESH
BF = jnp.bfloat16
F32 = jnp.float32


def al(value, multiple=128):
    return pl.multiple_of(value, multiple)


def kernel(amp, mask_in, bare, tiles, ids_in, eps_in, pair_in, out,
           amps, sfull, ssend, barep, bareo, inv, tr, grid, zr, xsend, xr, wf, op, rowe, mv, mask, ids, eps, pair,
           loc, sx, rx, sy, ry, sf, rf, sb, rb, so, ro, sm, rm, si, ri, st, rt, sz, rz, sw, rw, sa, ra, sd, rd):
    own, blk = lax.axis_index("own"), lax.axis_index("blk")
    core, z, xl = own % 2, (own // 2) % 8, own // 16
    xh, y = blk // 4, blk % 4

    def dev(xh_=None, y_=None, xl_=None, z_=None, core_=None):
        xh_ = xh if xh_ is None else xh_
        y_ = y if y_ is None else y_
        xl_ = xl if xl_ is None else xl_
        z_ = z if z_ is None else z_
        core_ = core if core_ is None else core_
        return {"own": xl_ * 16 + z_ * 2 + core_, "blk": xh_ * 4 + y_}

    def remote(src, dst, send, recv, device):
        return pltpu.make_async_remote_copy(
            src_ref=src, dst_ref=dst, send_sem=send, recv_sem=recv,
            device_id=device, device_id_type=MESH)

    other = dev(xh_=1 - xh)
    sibling = dev(core_=1 - core)
    yn = [dev(y_=(y + 1) % 4), dev(y_=(y + 3) % 4)]
    zk = [dev(z_=(z + k) % 8) for k in range(1, 8)]
    zn = [zk[0], zk[6]]
    xs = [dev(xl_=1 - xl), other, dev(xh_=1 - xh, xl_=1 - xl)]
    quad = [sibling, dev(xl_=1 - xl), dev(xl_=1 - xl, core_=1 - core)]
    quarter = core * 2 + xl
    quarters = [(1 - core) * 2 + xl, core * 2 + 1 - xl, (1 - core) * 2 + 1 - xl]

    mine, theirs = al(xh * HALF), al((1 - xh) * HALF)
    load_theirs = pltpu.make_async_copy(amp.at[:, pl.ds(theirs, HALF)], amps.at[:, pl.ds(0, HALF)], loc.at[0])
    load_mine = pltpu.make_async_copy(amp.at[:, pl.ds(mine, HALF)], amps.at[:, pl.ds(HALF, HALF)], loc.at[1])
    load_bare = pltpu.make_async_copy(bare.at[:, pl.ds(mine, HALF)], bareo, loc.at[2])
    load_tiles = pltpu.make_async_copy(
        tiles.at[:, pl.ds(al(quarter * QR, QR), QR), :], tr.at[0, pl.ds(0, SLOTS)], loc.at[3])
    load_ids = pltpu.make_async_copy(ids_in, ids, loc.at[4])
    load_mask = pltpu.make_async_copy(mask_in, mask, loc.at[5])
    load_eps = pltpu.make_async_copy(eps_in, eps, loc.at[6])
    load_pair = pltpu.make_async_copy(pair_in, pair, loc.at[7])

    barrier = pltpu.get_barrier_semaphore()
    peers = yn + zk + xs + [sibling, quad[2]]
    for peer in peers:
        pl.semaphore_signal(barrier, inc=1, device_id=peer, device_id_type=MESH)
    for load in (load_ids, load_mask, load_theirs, load_mine, load_tiles, load_eps, load_pair, load_bare):
        load.start()
    load_ids.wait()

    def invert(q, _):
        slot = SLOTS
        for s in range(SLOTS):
            slot = jnp.where(ids[s] == q, s, slot)
        inv[0, q] = slot
        return 0

    lax.fori_loop(0, 3 * NT, invert, 0)
    pl.semaphore_wait(barrier, len(peers))

    def rows_of(xh_, y_):
        return pl.ds(al((xh_ * 4 + y_) * ROWS), ROWS)

    def part(n, base=0):
        if isinstance(n, int):
            return pl.ds(al(base + STARTS[n]), WIDTHS[n])
        return pl.ds(al(base + n * WIDE), WIDE)

    def x_copy(n):
        return remote(ssend.at[:, part(n)], sfull.at[rows_of(xh, y), part(n)], sx.at[n], rx.at[n], other)

    def y_copy(b, d, n):
        where = sfull.at[rows_of(xh if b == 0 else 1 - xh, y), part(n)]
        return remote(where, where, sy.at[b, d, n], ry.at[b, d, n], yn[d])

    def f_copy(d, n):
        where = sfull.at[rows_of(xh if d == 0 else 1 - xh, (y + 3) % 4 if d == 0 else (y + 1) % 4), part(n)]
        return remote(where, where, sf.at[d, n], rf.at[d, n], yn[d])

    def b_copy(n):
        return remote(bare.at[:, part(n, theirs)], barep.at[:, part(n)], sb.at[n], rb.at[n], other)

    def o_copy(n):
        return remote(op.at[:, part(n)], out.at[:, part(n, mine)], so.at[n], ro.at[n], other)

    def t_copy(j):
        return remote(tiles.at[:, pl.ds(al(quarters[j] * QR, QR), QR), :], tr.at[j + 1, pl.ds(0, SLOTS)], st.at[j], rt.at[j], quad[j])

    def i_copy(j):
        return remote(inv.at[0], inv.at[j + 1], si.at[j], ri.at[j], quad[j])

    for j in range(3):
        t_copy(j).start()
        i_copy(j).start()

    def screen(n, send=True):
        count = WIDTHS[n] // TILE
        for side in range(2):
            first = (1 - xh) if side == 0 else xh
            for c in range(count):
                here = STARTS[n] + c * TILE
                for r in range(3):
                    keep = mask[r, 0, first * (NT // 2) + here // TILE]
                    tile = amps[r * TILE:(r + 1) * TILE, side * HALF + here:side * HALF + here + TILE]
                    tile = jnp.where(keep > 0, tile, jnp.zeros_like(tile))
                    if side == 0:
                        ssend[r * TILE:(r + 1) * TILE, here:here + TILE] = tile
                    else:
                        sfull[pl.ds(al(blk * ROWS + r * TILE), TILE), here:here + TILE] = tile
            if side == 0 and send:
                x_copy(n).start()
        y_copy(0, 0, n).start()
        y_copy(0, 1, n).start()

    load_mask.wait()
    load_theirs.wait()
    load_mine.wait()
    for n in range(4):
        screen(n)
    b_copy(0).start()

    load_tiles.wait()
    for j in range(4):
        tr[j, SLOTS] = jnp.zeros((QR, TILE), BF)
    for j in range(3):
        t_copy(j).wait_recv()
        i_copy(j).wait_recv()

    def place(q, _):
        tile = tr[0, inv[0, q]]
        for j in range(1, 4):
            tile = tile + tr[j, inv[j, q]]
        grid[pl.ds(al(q // NT * QR, QR), QR), pl.ds(al(q % NT * TILE), TILE)] = tile
        return 0

    lax.fori_loop(0, 3 * NT, place, 0)
    here = pl.ds(al(z * ZC), ZC)

    def z_copy(k):
        return remote(grid.at[:, pl.ds(al((z + k) % 8 * ZC), ZC)], zr.at[k - 1], sz.at[k - 1], rz.at[k - 1], zk[k - 1])

    for k in (4, 3, 5, 2, 6, 1, 7):
        z_copy(k).start()

    for n in range(4, NC):
        screen(n, False)

    def spread_mask(c, _):
        for r in range(3):
            mv[1, r, pl.ds(c, 1), :] = jnp.full((1, TILE), mask[r, 0, c].astype(F32))
        return 0

    lax.fori_loop(0, NT, spread_mask, 0)
    m_copy = remote(mv.at[1], mv.at[0], sm, rm, other)
    m_copy.start()

    load_eps.wait()
    load_pair.wait()
    for side in range(2):
        for r in range(3):
            line = eps[pl.ds((side * 4 + y) * 3 + r, 1), :]
            rowe[side, r] = jnp.transpose(jnp.broadcast_to(line, (TILE, TILE)))

    def spread(n, both=False):
        x_copy(n).wait_recv()
        y_copy(1, 0, n).start()
        if both:
            y_copy(1, 1, n).start()
        y_copy(0, 0, n).wait_recv()
        f_copy(0, n).start()

    def partner_on(n):
        y_copy(1, 1, n).wait_recv()
        f_copy(1, n).start()
        if n + 2 < NC:
            y_copy(1, 1, n + 2).start()

    def w_copy(k):
        return remote(xsend, xr.at[k], sw.at[k], rw.at[k], xs[k])

    def reduce_z():
        for k in range(1, 8):
            z_copy(k).wait_recv()
        total = grid[:, here]
        for k in range(7):
            total = total + zr[k]
        xsend[...] = total
        for k in range(3):
            w_copy(k).start()

    def reduce_x():
        for k in range(3):
            w_copy(k).wait_recv()
        for r in range(3):
            rows = slice(r * QR, (r + 1) * QR)
            wf[xh, r, quarter, :, here] = xsend[rows, :]
            wf[xh, r, quarters[1], :, here] = xr[0, rows, :]
            wf[1 - xh, r, quarter, :, here] = xr[1, rows, :]
            wf[1 - xh, r, quarters[1], :, here] = xr[2, rows, :]

    def piece(g, z_, q=None):
        which = pl.ds(core * 2, 2) if q is None else pl.ds(core * 2 + q, 1)
        return wf.at[1 - xh if g == 0 else xh, :, which, :, pl.ds(al(z_ * ZC), ZC)]

    def from_z(d, s):
        return (z + 8 - s) % 8 if d == 0 else (z + s) % 8

    def a_copy(g, d, s):
        where = piece(g, from_z(d, s), d if s == 3 else None)
        return remote(where, where, sa.at[g, d, s], ra.at[g, d, s], zn[d])

    def d_copy(g, d, s):
        where = piece(g, from_z(d, s), d if s == 4 else None)
        return remote(where, where, sd.at[g, 4 * d + s], rd.at[g, 4 * d + s], sibling)

    def begin(g):
        a_copy(g, 0, 0).start()
        a_copy(g, 1, 0).start()
        d_copy(g, 0, 0).start()

    def onward(g, s):
        for d in range(2):
            a_copy(g, d, s - 1).wait_recv()
            if s < 4:
                a_copy(g, d, s).start()
            d_copy(g, d, s).start()

    def gathered(g):
        d_copy(g, 0, 0).wait_recv()
        for s in range(1, 5):
            for d in range(2):
                d_copy(g, d, s).wait_recv()

    spread(0, True)
    spread(1, True)
    spread(2)
    spread(3)
    reduce_z()
    for n in range(4, NC):
        x_copy(n).start()
    for n in range(1, NC):
        b_copy(n).start()
    reduce_x()
    begin(0)
    partner_on(0)
    spread(4)
    onward(0, 1)
    begin(1)
    spread(5)
    spread(6)
    partner_on(1)
    onward(0, 2)
    onward(1, 1)
    partner_on(2)
    onward(0, 3)
    onward(1, 2)
    onward(0, 4)
    load_bare.wait()
    m_copy.wait_recv()
    gathered(0)

    energy = pair[0]

    def rows_done(start, width, which):
        side = (1 - xh) if which == 0 else xh
        source = barep if which == 0 else bareo
        total = jnp.dot(wf[side].reshape(ROWS, NV), sfull[:, pl.ds(al(start), width)], preferred_element_type=F32)
        for c in range(width // TILE):
            at = pl.ds(al(start + c * TILE), TILE)
            column = xh * (NT // 2) + start // TILE + c
            line = eps[pl.ds(column, 1), :]
            for r in range(3):
                rows = slice(r * TILE, (r + 1) * TILE)
                denom = (rowe[side, r] + line) - energy
                value = source[rows, at].astype(F32) + total[rows, c * TILE:(c + 1) * TILE]
                value = (value / denom * mv[which, r, pl.ds(column, 1), :]).astype(BF)
                if which == 0:
                    op[rows, at] = value
                else:
                    out[rows, pl.ds(al(mine + start + c * TILE), TILE)] = value

    def theirs_done(n, start, width):
        y_copy(0, 1, n).wait_recv()
        y_copy(1, 0, n).wait_recv()
        f_copy(0, n).wait_recv()
        f_copy(1, n).wait_recv()
        b_copy(n).wait_recv()
        rows_done(start, width, 0)
        o_copy(n).start()

    def mine_done(n):
        rows_done(n * WIDE, WIDE, 1)

    for n in range(NC):
        theirs_done(n, STARTS[n], WIDTHS[n])
        if n == 0:
            partner_on(3)
            onward(1, 3)
        elif n == 1:
            onward(1, 4)
            gathered(1)
        elif n < 5:
            mine_done(n - 2)
            partner_on(n + 2)
            if n == 4:
                mine_done(3)
        elif n == 5:
            mine_done(4)
    mine_done(5)

    for j in range(3):
        t_copy(j).wait_send()
        i_copy(j).wait_send()
    m_copy.wait_send()
    for n in range(NC):
        x_copy(n).wait_send()
        b_copy(n).wait_send()
        for d in range(2):
            y_copy(0, d, n).wait_send()
            y_copy(1, d, n).wait_send()
            f_copy(d, n).wait_send()
    for k in range(1, 8):
        z_copy(k).wait_send()
    for k in range(3):
        w_copy(k).wait_send()
    for g in range(2):
        d_copy(g, 0, 0).wait_send()
        for d in range(2):
            for t in range(4):
                a_copy(g, d, t).wait_send()
                d_copy(g, d, t + 1).wait_send()
    for n in range(NC):
        o_copy(n).wait_send()
        o_copy(n).wait_recv()


def local(amplitudes, amp_mask, bare_ints, int_tiles, tile_ids, eps_virt, eps_pair):
    dma = pltpu.SemaphoreType.DMA
    vmem = pltpu.VMEM
    anywhere = pl.BlockSpec(memory_space=pl.ANY)
    inside = pl.BlockSpec(memory_space=pltpu.VMEM)
    sizes = [(NC,), (2, 2, NC), (2, NC), (NC,), (NC,)]
    sems = [dma(size) for size in sizes for _ in range(2)] + [dma, dma]
    sems += [dma(size) for size in [(3,), (3,), (7,), (3,), (2, 2, 4), (2, 9)] for _ in range(2)]
    result = pl.pallas_call(
        kernel,
        out_shape=vmem((ROWS, NV), BF),
        in_specs=[anywhere] * 7,
        out_specs=inside,
        scratch_shapes=[
            vmem((ROWS, NV), BF), vmem((NV, HALF), BF), vmem((ROWS, HALF), BF), vmem((ROWS, HALF), BF),
            vmem((ROWS, HALF), BF), pltpu.SMEM((4, TILE), jnp.int32), vmem((4, SLOTS + 1, QR, TILE), BF),
            vmem((3 * QR, NV), BF), vmem((7, 3 * QR, ZC), BF), vmem((3 * QR, ZC), BF), vmem((3, 3 * QR, ZC), BF),
            vmem((2, 3, 4, QR, NV), BF), vmem((ROWS, HALF), BF),
            vmem((2, 3, TILE, TILE), F32), vmem((2, 3, NT, TILE), F32),
            pltpu.SMEM((3, 1, NT), jnp.int32), pltpu.SMEM((SLOTS,), jnp.int32), vmem((NT, TILE), F32), pltpu.SMEM((1,), F32),
            dma((8,)), *sems,
        ],
        compiler_params=pltpu.CompilerParams(
            collective_id=0, has_side_effects=True, vmem_limit_bytes=56 * 1024 * 1024),
        name="cycle",
    )(amplitudes.reshape(ROWS, NV), amp_mask.reshape(3, 1, NT), bare_ints.reshape(ROWS, NV),
      int_tiles.reshape(SLOTS, TILE, TILE), tile_ids.reshape(SLOTS), eps_virt.reshape(NT, TILE), eps_pair)
    return result.reshape(1, ROWS, NV)


def solution(mesh):
    in_specs = (
        P("own", "blk", None),
        P("own", "blk", None),
        P("own", "blk", None),
        P("blk", "own", None, None, None),
        P("blk", "own", None),
        P(),
        P("own"),
    )
    return jax.shard_map(local, mesh=mesh, in_specs=in_specs, out_specs=P("own", "blk", None), check_vma=False)
```

```python
import jax
import jax.numpy as jnp
from jax import lax
from jax.experimental import pallas as pl
from jax.experimental.pallas import tpu as pltpu
from jax.sharding import PartitionSpec as P

TILE = 128
NT = 24
SLOTS = 10
ROWS = 384
NV = 3072
HALF = 1536
QR = 32
ZC = 384
STARTS = (0, 256, 512, 768, 1024, 1152, 1280, 1408)
WIDTHS = (256, 256, 256, 256, 128, 128, 128, 128)
NC = len(STARTS)
WIDE = 256
MESH = pl.DeviceIdType.MESH
BF = jnp.bfloat16
F32 = jnp.float32


def al(value, multiple=128):
    return pl.multiple_of(value, multiple)


def kernel(amp, mask_in, bare, tiles, ids_in, eps_in, pair_in, out,
           amps, sfull, ssend, barep, bareo, inv, tr, grid, zr, xsend, xr, wf, op, rowe, mv, mask, ids, eps, pair,
           loc, lx, sx, rx, sy, ry, sf, rf, sb, rb, so, ro, sm, rm, si, ri, st, rt, sz, rz, sw, rw, sa, ra, sd, rd):
    own, blk = lax.axis_index("own"), lax.axis_index("blk")
    core, z, xl = own % 2, (own // 2) % 8, own // 16
    xh, y = blk // 4, blk % 4

    def dev(xh_=None, y_=None, xl_=None, z_=None, core_=None):
        xh_ = xh if xh_ is None else xh_
        y_ = y if y_ is None else y_
        xl_ = xl if xl_ is None else xl_
        z_ = z if z_ is None else z_
        core_ = core if core_ is None else core_
        return {"own": xl_ * 16 + z_ * 2 + core_, "blk": xh_ * 4 + y_}

    def remote(src, dst, send, recv, device):
        return pltpu.make_async_remote_copy(
            src_ref=src, dst_ref=dst, send_sem=send, recv_sem=recv,
            device_id=device, device_id_type=MESH)

    other = dev(xh_=1 - xh)
    sibling = dev(core_=1 - core)
    yn = [dev(y_=(y + 1) % 4), dev(y_=(y + 3) % 4)]
    zk = [dev(z_=(z + k) % 8) for k in range(1, 8)]
    zn = [zk[0], zk[6]]
    xs = [dev(xl_=1 - xl), other, dev(xh_=1 - xh, xl_=1 - xl)]
    quad = [sibling, dev(xl_=1 - xl), dev(xl_=1 - xl, core_=1 - core)]
    quarter = core * 2 + xl
    quarters = [(1 - core) * 2 + xl, core * 2 + 1 - xl, (1 - core) * 2 + 1 - xl]

    mine, theirs = al(xh * HALF), al((1 - xh) * HALF)

    def load_amps(side, n):
        first = theirs if side == 0 else mine
        return pltpu.make_async_copy(
            amp.at[:, pl.ds(al(first + STARTS[n]), WIDTHS[n])],
            amps.at[:, pl.ds(side * HALF + STARTS[n], WIDTHS[n])], lx.at[side, n])

    load_bare = pltpu.make_async_copy(bare.at[:, pl.ds(mine, HALF)], bareo, loc.at[2])
    load_tiles = pltpu.make_async_copy(
        tiles.at[:, pl.ds(al(quarter * QR, QR), QR), :], tr.at[0, pl.ds(0, SLOTS)], loc.at[3])
    load_ids = pltpu.make_async_copy(ids_in, ids, loc.at[4])
    load_mask = pltpu.make_async_copy(mask_in, mask, loc.at[5])
    load_eps = pltpu.make_async_copy(eps_in, eps, loc.at[6])
    load_pair = pltpu.make_async_copy(pair_in, pair, loc.at[7])

    barrier = pltpu.get_barrier_semaphore()
    peers = yn + zk + xs + [sibling, quad[2]]
    for peer in peers:
        pl.semaphore_signal(barrier, inc=1, device_id=peer, device_id_type=MESH)
    load_mask.start()
    load_ids.start()
    for n in range(NC):
        for side in range(2):
            load_amps(side, n).start()
        if n == 1:
            load_tiles.start()
    for load in (load_eps, load_pair, load_bare):
        load.start()
    load_ids.wait()

    def invert(q, _):
        slot = SLOTS
        for s in range(SLOTS):
            slot = jnp.where(ids[s] == q, s, slot)
        inv[0, q] = slot
        return 0

    lax.fori_loop(0, 3 * NT, invert, 0)

    def screen(n):
        load_amps(0, n).wait()
        load_amps(1, n).wait()
        for side in range(2):
            first = (1 - xh) if side == 0 else xh
            for c in range(WIDTHS[n] // TILE):
                here = STARTS[n] + c * TILE
                for r in range(3):
                    keep = mask[r, 0, first * (NT // 2) + here // TILE]
                    tile = amps[r * TILE:(r + 1) * TILE, side * HALF + here:side * HALF + here + TILE]
                    tile = jnp.where(keep > 0, tile, jnp.zeros_like(tile))
                    if side == 0:
                        ssend[r * TILE:(r + 1) * TILE, here:here + TILE] = tile
                    else:
                        sfull[pl.ds(al(blk * ROWS + r * TILE), TILE), here:here + TILE] = tile

    load_mask.wait()
    screen(0)
    pl.semaphore_wait(barrier, len(peers))

    def rows_of(xh_, y_):
        return pl.ds(al((xh_ * 4 + y_) * ROWS), ROWS)

    def part(n, base=0):
        if isinstance(n, int):
            return pl.ds(al(base + STARTS[n]), WIDTHS[n])
        return pl.ds(al(base + n * WIDE), WIDE)

    def x_copy(n):
        return remote(ssend.at[:, part(n)], sfull.at[rows_of(xh, y), part(n)], sx.at[n], rx.at[n], other)

    def y_copy(b, d, n):
        where = sfull.at[rows_of(xh if b == 0 else 1 - xh, y), part(n)]
        return remote(where, where, sy.at[b, d, n], ry.at[b, d, n], yn[d])

    def f_copy(d, n):
        where = sfull.at[rows_of(xh if d == 0 else 1 - xh, (y + 3) % 4 if d == 0 else (y + 1) % 4), part(n)]
        return remote(where, where, sf.at[d, n], rf.at[d, n], yn[d])

    def b_copy(n):
        return remote(bare.at[:, part(n, theirs)], barep.at[:, part(n)], sb.at[n], rb.at[n], other)

    def o_copy(n):
        return remote(op.at[:, part(n)], out.at[:, part(n, mine)], so.at[n], ro.at[n], other)

    def t_copy(j):
        return remote(tiles.at[:, pl.ds(al(quarters[j] * QR, QR), QR), :], tr.at[j + 1, pl.ds(0, SLOTS)], st.at[j], rt.at[j], quad[j])

    def i_copy(j):
        return remote(inv.at[0], inv.at[j + 1], si.at[j], ri.at[j], quad[j])

    for j in range(3):
        t_copy(j).start()
        i_copy(j).start()

    def send(n, across=True):
        if across:
            x_copy(n).start()
        y_copy(0, 0, n).start()
        y_copy(0, 1, n).start()

    send(0)
    for n in range(1, 4):
        screen(n)
        send(n)
    b_copy(0).start()

    load_tiles.wait()
    for j in range(4):
        tr[j, SLOTS] = jnp.zeros((QR, TILE), BF)
    for j in range(3):
        t_copy(j).wait_recv()
        i_copy(j).wait_recv()

    def place(q, _):
        tile = tr[0, inv[0, q]]
        for j in range(1, 4):
            tile = tile + tr[j, inv[j, q]]
        grid[pl.ds(al(q // NT * QR, QR), QR), pl.ds(al(q % NT * TILE), TILE)] = tile
        return 0

    lax.fori_loop(0, 3 * NT, place, 0)
    here = pl.ds(al(z * ZC), ZC)

    def z_copy(k):
        return remote(grid.at[:, pl.ds(al((z + k) % 8 * ZC), ZC)], zr.at[k - 1], sz.at[k - 1], rz.at[k - 1], zk[k - 1])

    for k in (4, 3, 5, 2, 6, 1, 7):
        z_copy(k).start()

    for n in range(4, NC):
        screen(n)
        send(n, False)

    def spread_mask(c, _):
        for r in range(3):
            mv[1, r, pl.ds(c, 1), :] = jnp.full((1, TILE), mask[r, 0, c].astype(F32))
        return 0

    lax.fori_loop(0, NT, spread_mask, 0)
    m_copy = remote(mv.at[1], mv.at[0], sm, rm, other)
    m_copy.start()

    load_eps.wait()
    load_pair.wait()
    for side in range(2):
        for r in range(3):
            line = eps[pl.ds((side * 4 + y) * 3 + r, 1), :]
            rowe[side, r] = jnp.transpose(jnp.broadcast_to(line, (TILE, TILE)))

    def spread(n, both=False):
        x_copy(n).wait_recv()
        y_copy(1, 0, n).start()
        if both:
            y_copy(1, 1, n).start()
        y_copy(0, 0, n).wait_recv()
        f_copy(0, n).start()

    def partner_on(n):
        y_copy(1, 1, n).wait_recv()
        f_copy(1, n).start()
        if n + 2 < NC:
            y_copy(1, 1, n + 2).start()

    def w_copy(k):
        return remote(xsend, xr.at[k], sw.at[k], rw.at[k], xs[k])

    def reduce_z():
        for k in range(1, 8):
            z_copy(k).wait_recv()
        total = grid[:, here]
        for k in range(7):
            total = total + zr[k]
        xsend[...] = total
        for k in range(3):
            w_copy(k).start()

    def reduce_x():
        for k in range(3):
            w_copy(k).wait_recv()
        for r in range(3):
            rows = slice(r * QR, (r + 1) * QR)
            wf[xh, r, quarter, :, here] = xsend[rows, :]
            wf[xh, r, quarters[1], :, here] = xr[0, rows, :]
            wf[1 - xh, r, quarter, :, here] = xr[1, rows, :]
            wf[1 - xh, r, quarters[1], :, here] = xr[2, rows, :]

    def piece(g, z_, q=None):
        which = pl.ds(core * 2, 2) if q is None else pl.ds(core * 2 + q, 1)
        return wf.at[1 - xh if g == 0 else xh, :, which, :, pl.ds(al(z_ * ZC), ZC)]

    def from_z(d, s):
        return (z + 8 - s) % 8 if d == 0 else (z + s) % 8

    def a_copy(g, d, s):
        where = piece(g, from_z(d, s), d if s == 3 else None)
        return remote(where, where, sa.at[g, d, s], ra.at[g, d, s], zn[d])

    def d_copy(g, d, s):
        where = piece(g, from_z(d, s), d if s == 4 else None)
        return remote(where, where, sd.at[g, 4 * d + s], rd.at[g, 4 * d + s], sibling)

    def begin(g):
        a_copy(g, 0, 0).start()
        a_copy(g, 1, 0).start()
        d_copy(g, 0, 0).start()

    def onward(g, s):
        for d in range(2):
            a_copy(g, d, s - 1).wait_recv()
            if s < 4:
                a_copy(g, d, s).start()
            d_copy(g, d, s).start()

    def gathered(g):
        d_copy(g, 0, 0).wait_recv()
        for s in range(1, 5):
            for d in range(2):
                d_copy(g, d, s).wait_recv()

    spread(0, True)
    spread(1, True)
    spread(2)
    spread(3)
    reduce_z()
    for n in range(4, NC):
        x_copy(n).start()
    for n in range(1, NC):
        b_copy(n).start()
    reduce_x()
    begin(0)
    partner_on(0)
    spread(4)
    onward(0, 1)
    begin(1)
    spread(5)
    spread(6)
    spread(7)
    partner_on(1)
    onward(0, 2)
    onward(1, 1)
    partner_on(2)
    onward(0, 3)
    onward(1, 2)
    onward(0, 4)
    load_bare.wait()
    m_copy.wait_recv()
    gathered(0)

    energy = pair[0, 0]

    def rows_done(start, width, which, total=None):
        side = (1 - xh) if which == 0 else xh
        source = barep if which == 0 else bareo
        if total is None:
            total = jnp.dot(wf[side].reshape(ROWS, NV), sfull[:, pl.ds(al(start), width)], preferred_element_type=F32)
        for c in range(width // TILE):
            at = pl.ds(al(start + c * TILE), TILE)
            column = xh * (NT // 2) + start // TILE + c
            line = eps[pl.ds(column, 1), :]
            for r in range(3):
                rows = slice(r * TILE, (r + 1) * TILE)
                denom = (rowe[side, r] + line) - energy
                value = source[rows, at].astype(F32) + total[rows, c * TILE:(c + 1) * TILE]
                value = (value / denom * mv[which, r, pl.ds(column, 1), :]).astype(BF)
                if which == 0:
                    op[rows, at] = value
                else:
                    out[rows, pl.ds(al(mine + start + c * TILE), TILE)] = value

    def theirs_done(n, start, width):
        y_copy(0, 1, n).wait_recv()
        y_copy(1, 0, n).wait_recv()
        f_copy(0, n).wait_recv()
        f_copy(1, n).wait_recv()
        b_copy(n).wait_recv()
        rows_done(start, width, 0)
        o_copy(n).start()

    def mine_done(n):
        rows_done(n * WIDE, WIDE, 1)

    for n in range(NC - 1):
        theirs_done(n, STARTS[n], WIDTHS[n])
        if n == 0:
            partner_on(3)
            onward(1, 3)
        elif n == 1:
            onward(1, 4)
            gathered(1)
        elif n < 6:
            mine_done(n - 2)
            partner_on(n + 2)

    def sent(n):
        x_copy(n).wait_send()
        b_copy(n).wait_send()
        for d in range(2):
            y_copy(0, d, n).wait_send()
            y_copy(1, d, n).wait_send()
            f_copy(d, n).wait_send()

    for j in range(3):
        t_copy(j).wait_send()
        i_copy(j).wait_send()
    m_copy.wait_send()
    for n in range(NC - 2):
        sent(n)
    for k in range(1, 8):
        z_copy(k).wait_send()
    for k in range(3):
        w_copy(k).wait_send()
    for g in range(2):
        d_copy(g, 0, 0).wait_send()
        for d in range(2):
            for t in range(4):
                a_copy(g, d, t).wait_send()
                d_copy(g, d, t + 1).wait_send()

    last = NC - 1
    y_copy(0, 1, last).wait_recv()
    y_copy(1, 0, last).wait_recv()
    b_copy(last).wait_recv()

    def block_dot(xh_, y_):
        rows = rows_of(xh_, y_)
        return jnp.dot(wf[1 - xh, :, :, :, rows].reshape(ROWS, ROWS), sfull[rows, part(last)], preferred_element_type=F32)

    total = block_dot(0, y) + block_dot(1, y)
    for step in (1, 3):
        total = total + block_dot(0, (y + step) % 4) + block_dot(1, (y + step) % 4)
    for d in range(2):
        f_copy(d, last).wait_recv()
    for d in range(2):
        total = total + block_dot(d, (y + 2) % 4)
    rows_done(STARTS[last], WIDTHS[last], 0, total)
    o_copy(last).start()
    mine_done(4)
    mine_done(5)

    sent(NC - 2)
    sent(NC - 1)
    for n in range(NC):
        o_copy(n).wait_send()
        o_copy(n).wait_recv()


def local(amplitudes, amp_mask, bare_ints, int_tiles, tile_ids, eps_virt, eps_pair):
    dma = pltpu.SemaphoreType.DMA
    vmem = pltpu.VMEM
    anywhere = pl.BlockSpec(memory_space=pl.ANY)
    inside = pl.BlockSpec(memory_space=pltpu.VMEM)
    sizes = [(NC,), (2, 2, NC), (2, NC), (NC,), (NC,)]
    sems = [dma(size) for size in sizes for _ in range(2)] + [dma, dma]
    sems += [dma(size) for size in [(3,), (3,), (7,), (3,), (2, 2, 4), (2, 9)] for _ in range(2)]
    result = pl.pallas_call(
        kernel,
        out_shape=vmem((ROWS, NV), BF),
        in_specs=[anywhere] * 7,
        out_specs=inside,
        scratch_shapes=[
            vmem((ROWS, NV), BF), vmem((NV, HALF), BF), vmem((ROWS, HALF), BF), vmem((ROWS, HALF), BF),
            vmem((ROWS, HALF), BF), pltpu.SMEM((4, TILE), jnp.int32), vmem((4, SLOTS + 1, QR, TILE), BF),
            vmem((3 * QR, NV), BF), vmem((7, 3 * QR, ZC), BF), vmem((3 * QR, ZC), BF), vmem((3, 3 * QR, ZC), BF),
            vmem((2, 3, 4, QR, NV), BF), vmem((ROWS, HALF), BF),
            vmem((2, 3, TILE, TILE), F32), vmem((2, 3, NT, TILE), F32),
            pltpu.SMEM((3, 1, NT), jnp.int32), pltpu.SMEM((SLOTS,), jnp.int32), vmem((NT, TILE), F32), pltpu.SMEM((1, 1), F32),
            dma((8,)), dma((2, NC)), *sems,
        ],
        compiler_params=pltpu.CompilerParams(
            collective_id=0, has_side_effects=True, vmem_limit_bytes=56 * 1024 * 1024),
        name="cycle",
    )(amplitudes.reshape(ROWS, NV), amp_mask.reshape(3, 1, NT), bare_ints.reshape(ROWS, NV),
      int_tiles.reshape(SLOTS, TILE, TILE), tile_ids.reshape(SLOTS), eps_virt.reshape(NT, TILE), eps_pair.reshape(1, 1))
    return result.reshape(1, ROWS, NV)


def solution(mesh):
    in_specs = (
        P("own", "blk", None),
        P("own", "blk", None),
        P("own", "blk", None),
        P("blk", "own", None, None, None),
        P("blk", "own", None),
        P(),
        P("own"),
    )
    return jax.shard_map(local, mesh=mesh, in_specs=in_specs, out_specs=P("own", "blk", None), check_vma=False)
```
